32 devices in a mesh: fsdp: 4 (over z), tensor: 2 (over core), pool: 4 (over y, x).
Axes of the slice: x: 2, y: 2, z: 4, core: 2. Of those that a mesh axis runs over, the one named last changes fastest.
Arguments:
- hidden: bfloat16 [8192, 5120], P(('fsdp', 'pool'), 'tensor'), may hold values from -6 to 6
- queries: bfloat16 [8192, 5120], P(('fsdp', 'pool'), 'tensor'), may hold values from -200 to 200
- cotangent: bfloat16 [8192, 5120], P(('fsdp', 'pool'), 'tensor'), may hold values from -6 to 6
- segment: int32 [16, 512], P(('fsdp', 'pool')), may hold values from 0 to 15, never falling along the last dimension, each value on 1 to 384 neighbouring positions
- clip_mask: int32 [8192], P(('fsdp', 'pool')), may hold values 0 or 1
- rewards: float32 [256], P(('fsdp', 'pool')), may hold values from 0 to 1
- seq_order: int32 [256], P(('fsdp', 'pool')), may hold values from 0 to 255, each once
- kv_weight: float32 [5120, 2, 1024], P('fsdp', None, 'tensor'), may hold values from -0.078125 to 0.078125
- moment_one: float32 [5120, 2, 1024], P('fsdp', None, 'tensor'), may hold values from -60 to 60
- moment_two: float32 [5120, 2, 1024], P('fsdp', None, 'tensor'), may hold values from 1 to 10000
- dec_hidden: bfloat16 [128, 4, 5120], P(('fsdp', 'pool')), may hold values from -6 to 6
- dec_queries: bfloat16 [128, 4, 5120], P(('fsdp', 'pool'), None, 'tensor'), may hold values from -200 to 200
- kv_cache: bfloat16 [128, 256, 2, 1024], P(('fsdp', 'pool'), None, None, 'tensor'), may hold values from -6 to 6
- cache_len: int32 [128], P(('fsdp', 'pool')), may hold values from 1 to 256
Outputs:
- new_weight: float32 [5120, 2, 1024], P('fsdp', None, 'tensor')
- new_moment_one: float32 [5120, 2, 1024], P('fsdp', None, 'tensor')
- new_moment_two: float32 [5120, 2, 1024], P('fsdp', None, 'tensor')
- dec_out: bfloat16 [128, 4, 5120], P(('fsdp', 'pool'), None, 'tensor')
The draws below stay inside these ranges and needn't reach their ends.
Inputs may be any that keep to these rules, and one draw needn't show every extreme that they name: `segment`: each row never falls; every sequence number of a row has 1 to 384 tokens. `seq_order`: each place once.
All inputs are finite; a program needn't handle non-finite values. No bound on the sum of `clip_mask` on one device may be relied on, other than what follows from the above.
Results may differ from the reference program's by a relative error of at most 0.014.
The reference program's roundings to bfloat16 on the way count: a program that leaves them out, or rounds other values in their place, can miss the bound.
Values may be sent and summed in bfloat16 or wider, within the bound.
No kernel may reach another device: no remote copies, remote signals or barrier semaphores. Data moves between devices by JAX's collectives and lax.ppermute only.
A program may use at most 128 MiB of HBM per device.

```python
import math
import jax
import jax.numpy as jnp
import numpy as np
from jax import lax

D = 5120
QH = 40
KVH = 8
HD = 128
TOK_DEV = 512
GROUP = 16
CACHE = 256
STEPS = 4
SEQ_DEV = 16
SHARDS = 16
TOKENS = 8192
SEQS = 256
REQ = 128


def query_law(key, rows, columns):
    base = jax.random.normal(key, (rows, columns), jnp.float32)
    return jnp.clip(base, -200.0, 200.0)


def draw_queries(key, part):
    return query_law(jax.random.fold_in(key, 11), TOKENS, QH * HD).astype(jnp.bfloat16)


def draw_dec_queries(key, part):
    table = query_law(jax.random.fold_in(key, 13), REQ * STEPS, QH * HD)
    return table.reshape(REQ, STEPS, QH * HD).astype(jnp.bfloat16)


def with_ends(result, stream_key, low, high):
    place = [jax.random.randint(jax.random.fold_in(stream_key, axis), (), 0, length) for axis, length in enumerate(result.shape)]
    widest = result.shape.index(max(result.shape))
    next_to = place[:widest] + [(place[widest] + 1) % result.shape[widest]] + place[widest + 1:]
    return result.at[tuple(place)].set(low).at[tuple(next_to)].set(high)


def level_of(key, dims, cuts, least, top_value):
    gain = 1.0
    for dim, blocks in cuts:
        draws = jax.random.uniform(jax.random.fold_in(jax.random.fold_in(key, 6), dim), (blocks,), jnp.float32, least / len(cuts), top_value / len(cuts))
        gain = gain * jnp.repeat(jnp.exp(draws), dims[dim] // blocks).reshape((-1,) + (1,) * (len(dims) - 1 - dim))
    return gain


def profile(number_of, total, most, skew):
    portions = [(1 << 20) // math.isqrt(rank ** skew) + 1 for rank in range(2, number_of + 1)]
    spare, holding = total - most - (number_of - 1), [1] * (number_of - 1)
    while spare > 0:
        free = [i for i in range(number_of - 1) if holding[i] < most]
        pool, left = sum([portions[i] for i in free]), spare
        for i in free:
            extra = min(most - holding[i], max(1, left * portions[i] // pool), spare)
            holding[i] = holding[i] + extra
            spare = spare - extra
    return np.array([most] + holding)


def ragged(rng, count, total, most, lean):
    if count == 2:
        one = jax.random.randint(rng, (), max(1, total - most), min(most, total - 1) + 1)
        return jnp.stack([one, total - one])
    sizes = jnp.asarray(profile(count, total, most, lean), jnp.int32)
    twos = (count - 1) // 2
    giver, taker = sizes[1:1 + 2 * twos:2], sizes[2:2 + 2 * twos:2]
    room = jnp.minimum(giver - 1, most - taker)
    moved = jax.random.randint(jax.random.fold_in(rng, 1), (twos,), 0, 1 << 20) % (room + 1)
    sizes = sizes.at[1:1 + 2 * twos:2].set(giver - moved).at[2:2 + 2 * twos:2].set(taker + moved)
    return sizes[jax.random.permutation(jax.random.fold_in(rng, 2), count)]


def noise(own_key, extent, width, limit, cuts=(), kind=jnp.bfloat16):
    drawn = jax.random.normal(own_key, extent, jnp.float32) * width
    if len(cuts) > 0:
        drawn = level_of(own_key, extent, cuts, -0.22, 0.18) * drawn
    return jnp.clip(drawn, min=-limit, max=limit).astype(kind)


def setup_inputs(seed: int = 0) -> dict:
    splits = jax.random.split(jax.random.key(seed), 15)
    hidden = noise(splits[0], (TOKENS, D), 1.0, 6.0, ((0, 16), (1, 2)))
    queries = draw_queries(jax.random.fold_in(splits[14], 71), 0)
    cotangent = noise(splits[2], (TOKENS, QH * HD), 1.0, 6.0, ((0, 16), (1, 2)))
    segment = jax.vmap(lambda own: jnp.searchsorted(jnp.cumsum(ragged(own, SEQ_DEV, TOK_DEV, 3 * TOK_DEV // 4, 0)), jnp.arange(TOK_DEV), side="right"))(jax.random.split(splits[3], SHARDS)).reshape((SHARDS, TOK_DEV)).astype(jnp.int32)
    clip_mask = with_ends((jax.random.randint(splits[4], (TOKENS,), 0, 4) < 3).astype(jnp.int32), jax.random.fold_in(splits[4], 1), 0, 1)
    rewards = jnp.clip(1.0 * jax.random.uniform(splits[5], (SEQS,), jnp.float32) ** level_of(splits[5], (SEQS,), ((0, 16),), -0.2, 0.2), 0.0, 1.0)
    seq_order = jax.random.permutation(splits[6], SEQS).astype(jnp.int32)
    kv_weight = noise(splits[7], (D, 2, KVH * HD), D ** -0.5, 0.078125, ((0, 4), (2, 2)), jnp.float32)
    moment_one = noise(splits[8], (D, 2, KVH * HD), 10.0, 60.0, ((0, 4), (2, 2)), jnp.float32)
    moment_two = jnp.clip(jnp.exp(math.log(10000.0) - 9.2103404 * jax.random.uniform(splits[9], (D, 2, KVH * HD), jnp.float32) ** level_of(splits[9], (D, 2, KVH * HD), ((0, 4), (2, 2)), -0.2, 0.2)), 1.0, 10000.0)
    dec_hidden = noise(splits[10], (REQ, STEPS, D), 1.0, 6.0, ((0, 16),))
    dec_queries = draw_dec_queries(jax.random.fold_in(splits[14], 71), 0)
    kv_cache = noise(splits[12], (REQ, CACHE, 2, KVH * HD), 1.0, 6.0, ((0, 16), (3, 2)))
    cache_len = with_ends(jax.random.randint(splits[13], (REQ,), 1, CACHE + 1), jax.random.fold_in(splits[13], 1), 1, CACHE).astype(jnp.int32)
    return dict(hidden=hidden, queries=queries, cotangent=cotangent, segment=segment, clip_mask=clip_mask, rewards=rewards, seq_order=seq_order, kv_weight=kv_weight, moment_one=moment_one, moment_two=moment_two, dec_hidden=dec_hidden, dec_queries=dec_queries, kv_cache=kv_cache, cache_len=cache_len)


beta_one = 0.9
beta_two = 0.999
learn_rate = 0.001
weight_decay = 0.1
adam_epsilon = 1e-08
adam_step = 10.0
variance_floor = 0.04
masked_score = -1e+30

def rounded(value):
    return lax.optimization_barrier(value.astype(jnp.bfloat16)).astype(jnp.float32)

def learner_grads(keys_values, queries, cotangent, segment, coefficient):
    block_rows = queries.shape[0]
    head_size = queries.shape[3]
    score_scale = 1.0 / math.sqrt(head_size)
    key_rows = keys_values[:, 0].astype(jnp.float32)
    value_rows = keys_values[:, 1].astype(jnp.float32)
    query_full = queries.astype(jnp.float32)
    scores = jnp.einsum('thrd,uhd->hrtu', query_full, key_rows) * score_scale
    places = jnp.arange(block_rows)
    allowed = (segment[:, None] == segment[None, :]) & (places[None, :] <= places[:, None])
    scores = jnp.where(allowed, scores, masked_score)
    row_max = lax.optimization_barrier(jnp.max(scores, axis=-1, keepdims=True))
    weights = jnp.exp(scores - row_max)
    attention = weights / lax.optimization_barrier(jnp.sum(weights, axis=-1, keepdims=True))
    attention_low = rounded(attention)
    upstream = rounded(coefficient[:, None, None, None] * cotangent.astype(jnp.float32))
    grad_prob = jnp.einsum('thrd,uhd->hrtu', upstream, value_rows)
    row_inner = lax.optimization_barrier(jnp.sum(attention * grad_prob, axis=-1, keepdims=True))
    grad_score = rounded(attention * (grad_prob - row_inner) * score_scale)
    grad_values = jnp.einsum('hrtu,thrd->uhd', attention_low, upstream)
    grad_keys = jnp.einsum('hrtu,thrd->uhd', grad_score, query_full)
    return jnp.stack([grad_keys, grad_values], axis=1).astype(jnp.bfloat16)

def decode_attend(queries, cache, fresh, lengths):
    head_size = queries.shape[4]
    steps_here = queries.shape[1]
    capacity = cache.shape[1]
    score_scale = 1.0 / math.sqrt(head_size)
    query_full = queries.astype(jnp.float32)
    cached = jnp.einsum('bshqd,blhd->bshql', query_full, cache[:, :, 0].astype(jnp.float32)) * score_scale
    recent = jnp.einsum('bshqd,bjhd->bshqj', query_full, fresh[:, :, 0].astype(jnp.float32)) * score_scale
    live = jnp.arange(capacity)[None, :] < lengths[:, None]
    cached = jnp.where(live[:, None, None, None, :], cached, masked_score)
    before = jnp.arange(steps_here)[None, :] <= jnp.arange(steps_here)[:, None]
    recent = jnp.where(before[None, :, None, None, :], recent, masked_score)
    row_max = jnp.maximum(lax.optimization_barrier(jnp.max(cached, axis=-1, keepdims=True)), lax.optimization_barrier(jnp.max(recent, axis=-1, keepdims=True)))
    cached_exp = jnp.exp(cached - row_max)
    recent_exp = jnp.exp(recent - row_max)
    total = lax.optimization_barrier(jnp.sum(cached_exp, axis=-1, keepdims=True)) + lax.optimization_barrier(jnp.sum(recent_exp, axis=-1, keepdims=True))
    cached_low = rounded(cached_exp / total)
    recent_low = rounded(recent_exp / total)
    output = jnp.einsum('bshql,blhd->bshqd', cached_low, cache[:, :, 1].astype(jnp.float32))
    output = output + jnp.einsum('bshqj,bjhd->bshqd', recent_low, fresh[:, :, 1].astype(jnp.float32))
    return output.astype(jnp.bfloat16).reshape(queries.shape[0], steps_here, -1)

def reference(hidden, queries, cotangent, segment, clip_mask, rewards, seq_order, kv_weight, moment_one, moment_two, dec_hidden, dec_queries, kv_cache, cache_len):
    blocks = segment.shape[0]
    tok_rows = segment.shape[1]
    seq_rows = rewards.shape[0] // blocks
    groups_total = rewards.shape[0] // GROUP
    kv_width = kv_weight.shape[2]
    heads_kv = kv_width // HD
    head_ratio = QH // KVH
    group_of = seq_order // GROUP
    onehot = (group_of[:, None] == jnp.arange(groups_total, dtype=jnp.int32)[None, :]).astype(jnp.float32)
    stats = jnp.stack([rewards, rewards * rewards], axis=1)
    sums = lax.optimization_barrier(jnp.sum(onehot[:, :, None] * stats[:, None, :], axis=0))
    mean = sums[:, 0] / GROUP
    spread = sums[:, 1] / GROUP - mean * mean
    denom = jnp.sqrt(jnp.maximum(spread, variance_floor))
    advantage = (rewards - lax.optimization_barrier(jnp.sum(onehot * mean[None, :], axis=1))) / lax.optimization_barrier(jnp.sum(onehot * denom[None, :], axis=1))
    advantage_blocks = advantage.reshape(blocks, seq_rows)
    coefficient_all = jnp.take_along_axis(advantage_blocks, segment, axis=1).reshape(-1) * clip_mask.astype(jnp.float32)
    weight_low = kv_weight.astype(jnp.bfloat16).reshape(D, 2 * kv_width)

    def one_block(total, index):
        start = index * tok_rows
        rows = lax.dynamic_slice_in_dim(hidden, start, tok_rows, 0)
        projected = jnp.dot(rows, weight_low, preferred_element_type=jnp.float32)
        keys_values = projected.astype(jnp.bfloat16).reshape(tok_rows, 2, heads_kv, HD)
        query_rows = lax.dynamic_slice_in_dim(queries, start, tok_rows, 0).reshape(tok_rows, heads_kv, head_ratio, HD)
        cot_rows = lax.dynamic_slice_in_dim(cotangent, start, tok_rows, 0).reshape(tok_rows, heads_kv, head_ratio, HD)
        coef_rows = lax.dynamic_slice_in_dim(coefficient_all, start, tok_rows, 0)
        seg_rows = lax.dynamic_slice_in_dim(segment, index, 1, 0)[0]
        grad_kv = learner_grads(keys_values, query_rows, cot_rows, seg_rows, coef_rows).reshape(tok_rows, 2 * kv_width)
        partial_value = jnp.einsum('tc,tk->ck', rows, grad_kv, preferred_element_type=jnp.float32)
        return (total + rounded(partial_value), None)
    total, _ = lax.scan(one_block, jnp.zeros((D, 2 * kv_width), jnp.float32), jnp.arange(blocks, dtype=jnp.int32))
    grad = total.reshape(D, 2, kv_width)
    new_moment_one = beta_one * moment_one + (1.0 - beta_one) * grad
    new_moment_two = beta_two * moment_two + (1.0 - beta_two) * grad * grad
    first_hat = new_moment_one / (1.0 - beta_one ** adam_step)
    second_hat = new_moment_two / (1.0 - beta_two ** adam_step)
    new_weight = kv_weight - learn_rate * (first_hat / (jnp.sqrt(second_hat) + adam_epsilon) + weight_decay * kv_weight)
    req_total = dec_hidden.shape[0]
    steps_here = dec_hidden.shape[1]
    capacity = kv_cache.shape[1]
    rollout_low = new_weight.astype(jnp.bfloat16).reshape(D, 2 * kv_width)
    fresh = jnp.dot(dec_hidden.reshape(req_total * steps_here, D), rollout_low, preferred_element_type=jnp.float32)
    fresh = fresh.astype(jnp.bfloat16).reshape(req_total, steps_here, 2, heads_kv, HD)
    cache = kv_cache.reshape(req_total, capacity, 2, heads_kv, HD)
    query_dec = dec_queries.reshape(req_total, steps_here, heads_kv, head_ratio, HD)
    dec_out = decode_attend(query_dec, cache, fresh, cache_len)
    return (new_weight, new_moment_one, new_moment_two, dec_out)
```

```python
import functools
import math

import jax
import jax.numpy as jnp
from jax import lax
from jax.experimental import pallas as pl
from jax.experimental.pallas import tpu as pltpu
from jax.sharding import PartitionSpec as P

D = 5120
QH = 40
KVH = 8
HD = 128
GROUP = 16
RATIO = QH // KVH

beta_one = 0.9
beta_two = 0.999
learn_rate = 0.001
weight_decay = 0.1
adam_epsilon = 1e-08
adam_step = 10.0
variance_floor = 0.04
masked_score = -1e30
score_scale = 1.0 / math.sqrt(HD)


MAX_CHUNKS = 2


def ring(n, s):
    return [(i, (i + s) % n) for i in range(n)]


def power_of_two(n):
    return n & (n - 1) == 0


def slot_index(k):
    n = lax.axis_size("pool")
    p = lax.axis_index("pool")
    return p ^ k if power_of_two(n) else lax.rem(p + k, n)


def from_slot(x, k):
    n = lax.axis_size("pool")
    perm = [(i, i ^ k) for i in range(n)] if power_of_two(n) else ring(n, -k)
    return lax.ppermute(x, "pool", perm)


def pool_gather(piece):
    n = lax.axis_size("pool")
    if n != 4:
        return [piece] + [from_slot(piece, k) for k in range(1, n)]
    one = from_slot(piece, 1)
    two = from_slot(piece, 2)
    half = piece.shape[0] // 2
    low = from_slot(two[:half], 1)
    high = from_slot(one[half:], 2)
    return [piece, one, two, (low, high)]


def place(slots, rows):
    total = jnp.zeros((rows * len(slots),) + slots[0].shape[1:], slots[0].dtype)
    for k, slot in enumerate(slots):
        start = slot_index(k) * rows
        for part in slot if isinstance(slot, tuple) else (slot,):
            total = lax.dynamic_update_slice_in_dim(total, part, start, 0)
            start = start + part.shape[0]
    return total


def attention_kernel(q_ref, c_ref, k_ref, v_ref, coef_ref, segr_ref, segc_ref, out_ref, dk, dv):
    rows = k_ref.shape[0]
    heads = out_ref.shape[1] // (2 * HD)
    block = min(128, rows)
    head = pl.program_id(0)
    dk[...] = jnp.zeros_like(dk)
    dv[...] = jnp.zeros_like(dv)
    contract_last = (((1,), (1,)), ((), ()))
    for i in range(rows // block):
        low, high = i * block, (i + 1) * block
        allowed = (segc_ref[:high, :] == segr_ref[:, low:high]) & (
            lax.broadcasted_iota(jnp.int32, (high, block), 0)
            <= lax.broadcasted_iota(jnp.int32, (high, block), 1) + low
        )
        keys = k_ref[:high, :]
        values = v_ref[:high, :]
        coef = coef_ref[low:high, :]
        for r in range(RATIO):
            query = q_ref[low:high, r * HD : (r + 1) * HD]
            upstream = (coef * c_ref[low:high, r * HD : (r + 1) * HD].astype(jnp.float32)).astype(
                jnp.bfloat16
            )
            scores = (
                lax.dot_general(keys, query, contract_last, preferred_element_type=jnp.float32)
                * score_scale
            )
            scores = jnp.where(allowed, scores, masked_score)
            weights = jnp.exp(scores - jnp.max(scores, axis=0, keepdims=True))
            attention = weights * (1.0 / jnp.sum(weights, axis=0, keepdims=True))
            grad_prob = lax.dot_general(
                values, upstream, contract_last, preferred_element_type=jnp.float32
            )
            inner = jnp.sum(attention * grad_prob, axis=0, keepdims=True)
            grad_score = (attention * (grad_prob - inner) * score_scale).astype(jnp.bfloat16)
            dv[:high, :] += jnp.dot(
                attention.astype(jnp.bfloat16), upstream, preferred_element_type=jnp.float32
            )
            dk[:high, :] += jnp.dot(grad_score, query, preferred_element_type=jnp.float32)
    at = pl.multiple_of(head * HD, HD)
    out_ref[:, pl.ds(at, HD)] = dk[...].astype(jnp.bfloat16)
    out_ref[:, pl.ds(pl.multiple_of(heads * HD + at, HD), HD)] = dv[...].astype(jnp.bfloat16)


def learner_grads(kv, queries, cotangent, coefficient, segment, first, heads):
    rows = kv.shape[0]
    wide = RATIO * HD
    return pl.pallas_call(
        attention_kernel,
        grid=(heads,),
        in_specs=[
            pl.BlockSpec((rows, wide), lambda h: (0, first + h)),
            pl.BlockSpec((rows, wide), lambda h: (0, first + h)),
            pl.BlockSpec((rows, HD), lambda h: (0, h)),
            pl.BlockSpec((rows, HD), lambda h: (0, heads + h)),
            pl.BlockSpec((rows, 1), lambda h: (0, 0)),
            pl.BlockSpec((1, rows), lambda h: (0, 0)),
            pl.BlockSpec((rows, 1), lambda h: (0, 0)),
        ],
        out_specs=pl.BlockSpec((rows, 2 * heads * HD), lambda h: (0, 0)),
        out_shape=jax.ShapeDtypeStruct((rows, 2 * heads * HD), jnp.bfloat16),
        scratch_shapes=[pltpu.VMEM((rows, HD), jnp.float32), pltpu.VMEM((rows, HD), jnp.float32)],
        compiler_params=pltpu.CompilerParams(vmem_limit_bytes=24 << 20),
        cost_estimate=pl.CostEstimate(
            flops=10 * heads * RATIO * rows * rows * HD,
            bytes_accessed=heads * rows * HD * 4 * (RATIO + 2),
            transcendentals=heads * RATIO * rows * rows,
        ),
        name="learner_grads",
    )(
        queries,
        cotangent,
        kv,
        kv,
        coefficient.reshape(rows, 1),
        segment.reshape(1, rows),
        segment.reshape(rows, 1),
    )


def cached_part(queries, cache, lengths):
    capacity = cache.shape[1]
    scores = (
        jnp.einsum("bshqd,blhd->bhqsl", queries, cache[:, :, 0], preferred_element_type=jnp.float32)
        * score_scale
    )
    live = jnp.arange(capacity)[None, :] < lengths[:, None]
    scores = jnp.where(live[:, None, None, None, :], scores, masked_score)
    top = jnp.max(scores, axis=-1, keepdims=True)
    weights = jnp.exp(scores - top)
    total = jnp.sum(weights, axis=-1, keepdims=True)
    mixed = jnp.einsum(
        "bhqsl,blhd->bhqsd",
        weights.astype(jnp.bfloat16),
        cache[:, :, 1],
        preferred_element_type=jnp.float32,
    )
    return top, total, mixed


def decode_kernel(q_ref, f_ref, top_ref, total_ref, mixed_ref, out_ref, *, steps):
    rows = q_ref.shape[0]
    heads = top_ref.shape[0]
    wide = RATIO * rows
    row = lax.rem(lax.broadcasted_iota(jnp.int32, (wide, rows), 0), rows)
    col = lax.broadcasted_iota(jnp.int32, (wide, rows), 1)
    allowed = (row // steps == col // steps) & (col <= row)
    for h in range(heads):
        query = jnp.concatenate(
            [q_ref[:, (h * RATIO + r) * HD : (h * RATIO + r + 1) * HD] for r in range(RATIO)], axis=0
        )
        scores = (
            lax.dot_general(
                query,
                f_ref[:, h * HD : (h + 1) * HD],
                (((1,), (1,)), ((), ())),
                preferred_element_type=jnp.float32,
            )
            * score_scale
        )
        scores = jnp.where(allowed, scores, masked_score)
        top = top_ref[h]
        new_top = jnp.maximum(top, jnp.max(scores, axis=1, keepdims=True))
        recent = jnp.exp(scores - new_top)
        shrink = jnp.exp(top - new_top)
        total = total_ref[h] * shrink + jnp.sum(recent, axis=1, keepdims=True)
        output = mixed_ref[h] * shrink + jnp.dot(
            recent.astype(jnp.bfloat16),
            f_ref[:, (heads + h) * HD : (heads + h + 1) * HD],
            preferred_element_type=jnp.float32,
        )
        output = (output / total).astype(jnp.bfloat16)
        for r in range(RATIO):
            out_ref[:, (h * RATIO + r) * HD : (h * RATIO + r + 1) * HD] = output[
                r * rows : (r + 1) * rows, :
            ]


def decode_merge(queries, fresh, top, total, mixed, steps):
    return pl.pallas_call(
        functools.partial(decode_kernel, steps=steps),
        out_shape=jax.ShapeDtypeStruct(queries.shape, jnp.bfloat16),
        name="decode_merge",
    )(queries, fresh, top, total, mixed)


def group_sums(partial):
    for axis in ("pool", "fsdp"):
        n = lax.axis_size(axis)
        if not power_of_two(n):
            partial = lax.psum(partial, axis)
            continue
        step = 1
        while step < n:
            partial = partial + lax.ppermute(partial, axis, [(i, i ^ step) for i in range(n)])
            step *= 2
    return partial


def body(
    hidden,
    queries,
    cotangent,
    segment,
    clip_mask,
    rewards,
    seq_order,
    kv_weight,
    moment_one,
    moment_two,
    dec_hidden,
    dec_queries,
    kv_cache,
    cache_len,
):
    nf = lax.axis_size("fsdp")
    nt = lax.axis_size("tensor")
    np_ = lax.axis_size("pool")
    f = lax.axis_index("fsdp")
    t = lax.axis_index("tensor")
    p = lax.axis_index("pool")
    per = nf // nt
    block_rows = hidden.shape[0]
    row_count, _, kv_width = kv_weight.shape
    quarter = row_count // np_
    heads_here = kv_width // HD
    chunks = min(MAX_CHUNKS, heads_here)
    heads = heads_here // chunks
    cols = heads * HD

    def column_chunk(x, c):
        return x[:, :, c * cols : (c + 1) * cols].reshape(x.shape[0], 2 * cols)

    own_rows = lax.dynamic_slice_in_dim(kv_weight, p * quarter, quarter, 0).astype(jnp.bfloat16)
    weight_low = kv_weight.astype(jnp.bfloat16)
    tokens = [hidden]
    for _ in range(nt - 1):
        tokens.append(lax.ppermute(tokens[-1], "tensor", ring(nt, -1)))
    tokens = jnp.stack(tokens)

    def features(shard):
        half = lax.rem(lax.div(shard, per) - t + nt, nt)
        start = lax.rem(shard, per) * row_count
        return lax.dynamic_slice(
            tokens, (half, jnp.int32(0), start), (1, block_rows, row_count)
        )[0]

    turned = hidden.T.reshape(per, np_, quarter, block_rows)
    hid = []
    for k in range(np_):
        piece = lax.dynamic_index_in_dim(turned, slot_index(k), 1, keepdims=False)
        hid.append(piece if k == 0 else from_slot(piece, k))
    hid_all = []
    for piece in hid:
        parts = [piece]
        for _ in range(nt - 1):
            parts.append(lax.ppermute(parts[-1], "tensor", ring(nt, -1)))
        hid_all.append(jnp.concatenate(parts, axis=0).reshape(nf * quarter, block_rows))

    shards = nf * np_
    groups_total = rewards.shape[0] * shards // GROUP
    group_of = seq_order // GROUP
    onehot = (group_of[:, None] == jnp.arange(groups_total, dtype=jnp.int32)[None, :]).astype(
        jnp.float32
    )
    stats = jnp.stack([rewards, rewards * rewards], axis=1)
    sums = group_sums(jnp.sum(onehot[:, :, None] * stats[:, None, :], axis=0))
    mean = sums[:, 0] / GROUP
    spread = sums[:, 1] / GROUP - mean * mean
    denom = jnp.sqrt(jnp.maximum(spread, variance_floor))
    advantage = (rewards - jnp.sum(onehot * mean[None, :], axis=1)) / jnp.sum(
        onehot * denom[None, :], axis=1
    )
    local_seg = segment[0]
    member = (local_seg[:, None] == jnp.arange(rewards.shape[0], dtype=jnp.int32)[None, :]).astype(
        jnp.float32
    )
    coefficient = jnp.sum(member * advantage[None, :], axis=1) * clip_mask.astype(jnp.float32)

    dec_rows, steps, _ = dec_hidden.shape
    flat_rows = dec_rows * steps
    dec_flat = dec_hidden.reshape(flat_rows, dec_hidden.shape[2])
    dec_parts = []
    for s in range(nf):
        target = lax.rem(f + s, nf)
        piece = lax.dynamic_slice_in_dim(dec_flat, target * row_count, row_count, 1)
        dec_parts.append(piece if s == 0 else lax.ppermute(piece, "fsdp", ring(nf, s)))
    dec_stack = jnp.concatenate(dec_parts, axis=0)
    query_dec = dec_queries.reshape(dec_rows, steps, heads_here, RATIO, HD)
    cache = kv_cache.reshape(dec_rows, kv_cache.shape[1], 2, heads_here, HD)
    top, total, mixed = cached_part(query_dec, cache, cache_len)

    def by_head(x):
        return jnp.transpose(x, (1, 2, 0, 3, 4)).reshape(heads_here, RATIO * flat_rows, x.shape[4])

    top, total, mixed = by_head(top), by_head(total), by_head(mixed)
    dec_query_flat = dec_queries.reshape(flat_rows, dec_queries.shape[2])

    grads = []
    dec_outs = []
    for c in range(chunks):
        piece = column_chunk(own_rows, c)
        projected = jnp.dot(
            features(f), column_chunk(weight_low, c), preferred_element_type=jnp.float32
        )
        for s in range(1, nf):
            piece = lax.ppermute(piece, "fsdp", ring(nf, 1))
            gathered = place(pool_gather(piece), quarter)
            projected = projected + jnp.dot(
                features(lax.rem(f - s + nf, nf)), gathered, preferred_element_type=jnp.float32
            )
        keys_values = projected.astype(jnp.bfloat16)
        grad_kv = learner_grads(
            keys_values, queries, cotangent, coefficient, local_seg, c * heads, heads
        )

        partial = None
        for k, slot in enumerate(pool_gather(grad_kv)):
            slot = jnp.concatenate(slot, axis=0) if isinstance(slot, tuple) else slot
            product = jnp.dot(hid_all[k], slot, preferred_element_type=jnp.float32)
            partial = product if partial is None else partial + product

        def rows_for(shard):
            half = lax.rem(lax.div(shard, per) - t + nt, nt)
            start = (half * per + lax.rem(shard, per)) * quarter
            return lax.dynamic_slice_in_dim(partial, start, quarter, 0)

        running = rows_for(lax.rem(f + nf - 1, nf))
        for s in range(1, nf):
            running = lax.ppermute(running.astype(jnp.bfloat16), "fsdp", ring(nf, 1))
            running = running.astype(jnp.float32) + rows_for(lax.rem(f + 2 * nf - 1 - s, nf))
        own_grad = running.astype(jnp.bfloat16)
        grad = place(pool_gather(own_grad), quarter)
        grads.append(grad.reshape(row_count, 2, cols))

        width = slice(c * cols, (c + 1) * cols)
        rollout = update(
            kv_weight[:, :, width], moment_one[:, :, width], moment_two[:, :, width], grads[c]
        )[0].astype(jnp.bfloat16)
        product = jnp.dot(
            dec_stack, rollout.reshape(row_count, 2 * cols), preferred_element_type=jnp.float32
        ).reshape(nf, flat_rows, 2 * cols)
        fresh = product[0]
        for s in range(1, nf):
            fresh = fresh + lax.ppermute(product[s], "fsdp", ring(nf, -s))
        here = slice(c * heads, (c + 1) * heads)
        dec_outs.append(
            decode_merge(
                dec_query_flat[:, c * heads * RATIO * HD : (c + 1) * heads * RATIO * HD],
                fresh.astype(jnp.bfloat16),
                top[here],
                total[here],
                mixed[here],
                steps,
            )
        )

    grad_full = jnp.concatenate(grads, axis=2) if chunks > 1 else grads[0]
    new_weight, new_moment_one, new_moment_two = update(
        kv_weight, moment_one, moment_two, grad_full
    )
    dec_out = jnp.concatenate(dec_outs, axis=1) if chunks > 1 else dec_outs[0]
    return (
        new_weight,
        new_moment_one,
        new_moment_two,
        dec_out.reshape(dec_rows, steps, dec_out.shape[1]),
    )


def update(weight, moment_one, moment_two, grad):
    grad = grad.astype(jnp.float32)
    new_moment_one = beta_one * moment_one + (1.0 - beta_one) * grad
    new_moment_two = beta_two * moment_two + (1.0 - beta_two) * grad * grad
    first_hat = new_moment_one / (1.0 - beta_one**adam_step)
    second_hat = new_moment_two / (1.0 - beta_two**adam_step)
    new_weight = weight - learn_rate * (
        first_hat / (jnp.sqrt(second_hat) + adam_epsilon) + weight_decay * weight
    )
    return new_weight, new_moment_one, new_moment_two


def solution(mesh):
    return jax.shard_map(
        body,
        mesh=mesh,
        in_specs=(
            P(("fsdp", "pool"), "tensor"),
            P(("fsdp", "pool"), "tensor"),
            P(("fsdp", "pool"), "tensor"),
            P(("fsdp", "pool"), None),
            P(("fsdp", "pool")),
            P(("fsdp", "pool")),
            P(("fsdp", "pool")),
            P("fsdp", None, "tensor"),
            P("fsdp", None, "tensor"),
            P("fsdp", None, "tensor"),
            P(("fsdp", "pool"), None, None),
            P(("fsdp", "pool"), None, "tensor"),
            P(("fsdp", "pool"), None, None, "tensor"),
            P(("fsdp", "pool")),
        ),
        out_specs=(
            P("fsdp", None, "tensor"),
            P("fsdp", None, "tensor"),
            P("fsdp", None, "tensor"),
            P(("fsdp", "pool"), None, "tensor"),
        ),
        check_vma=False,
    )
```
